512 devices in a mesh: row: 16 (over y, x_hi), col: 32 (over z, x_lo, core).
Axes of the slice: x: 4 (x_hi: 2, x_lo: 2; x = x_hi * 2 + x_lo), y: 8, z: 8, core: 2. Of those that a mesh axis runs over, the one named last changes fastest.
Arguments:
- sigma_anc: bfloat16 [4096, 4096], P('row', 'col'), as said below
- structure: int32 [512, 4], P(('row', 'col')), may hold values from 0 to 15, all different within a row
- factor: bfloat16 [512, 1024, 1024], P(('row', 'col')), may hold values from -0.375 to 0.375
- diag_term: float32 [512, 1024], P(('row', 'col')), may hold values from 1 to 8
Outputs:
- sigma_off: bfloat16 [512, 1024, 1024], P(('row', 'col'))
- variances: float32 [512, 1024], P(('row', 'col'))
The draws below stay inside these ranges and needn't reach their ends.
Inputs may be any that keep to these rules, and one draw needn't show every extreme that they name: `structure`: each row names 4 different ancestor blocks, and every ancestor block is named by some row. sigma_anc is exactly symmetric, as the inverse of a symmetric precision matrix: its entry (p, q) equals its entry (q, p) bit for bit.
All inputs are finite; a program needn't handle non-finite values.
Results may differ from the reference program's by a relative error of at most 0.001.
Values may be sent and summed in bfloat16 or wider, within the bound.
No kernel may reach another device: no remote copies, remote signals or barrier semaphores. Data moves between devices by JAX's collectives and lax.ppermute only.
A program may use at most 64 MiB of HBM per device.

```python
import math
import jax
import jax.numpy as jnp
from jax import lax

B = 256
W = 1024
S = 4
NA = 16
NS = 512


def draw_sigma_anc(key, part):
    total = NA * B
    first_key, second_key = jax.random.split(jax.random.fold_in(key, 17))
    raw_values = jax.random.normal(first_key, (total, total), jnp.float32)
    diagonal_values = jax.random.uniform(second_key, (total,), jnp.float32, 1.0, 2.0)
    symmetric = (raw_values + raw_values.T) * (0.7071 / total ** 0.5)
    return (symmetric + jnp.diag(diagonal_values)).astype(jnp.bfloat16)


def block_scale(own_key, shape, pieces, smallest, largest):
    loudness = 1.0
    for dim, shards_of in pieces:
        draws = jax.random.uniform(jax.random.fold_in(jax.random.fold_in(own_key, 6), dim), (shards_of,), jnp.float32, smallest / len(pieces), largest / len(pieces))
        loudness = loudness * jnp.repeat(jnp.exp(draws), shape[dim] // shards_of).reshape((-1,) + (1,) * (len(shape) - 1 - dim))
    return loudness


def distinct(rng, rows, amount, top, lift):
    sequence = jax.random.permutation(jax.random.fold_in(rng, 1), amount)
    favour = sequence
    for power in range(3):
        favour = favour * favour // amount
    favour = favour * lift // amount
    lots = jax.random.randint(jax.random.fold_in(rng, 2), (rows, amount), 0, 4096) + favour
    fixed_rows = jax.random.permutation(jax.random.fold_in(rng, 3), rows)[jnp.arange(amount) % rows]
    lots = jnp.where(jnp.arange(rows)[:, None] == fixed_rows[None, :], 1 << 14, lots)
    merit = lots * amount + jnp.arange(amount)
    return lax.top_k(merit.astype(jnp.int32), top)[1].astype(jnp.int32)


def noise(own_key, extent, spread, limit, shards=(), dtype=jnp.bfloat16):
    level = block_scale(own_key, extent, shards, -0.22, 0.18) if shards else 1.0
    result = jax.random.normal(own_key, extent, jnp.float32) * spread * level
    return jnp.minimum(jnp.maximum(result, -limit), limit).astype(dtype)


def setup_inputs(seed: int = 0) -> dict:
    key_list = jax.random.split(jax.random.key(seed), 5)
    sigma_anc = draw_sigma_anc(jax.random.fold_in(key_list[4], 71), 0)
    structure = distinct(key_list[1], NS, NA, S, 4096)
    factor = noise(key_list[2], (NS, S * B, W), (S * B // 4) ** -0.5, 0.375, ((0, 512),))
    diag_term = jnp.clip(jnp.exp(math.log(8.0) - 2.0794415 * jax.random.uniform(key_list[3], (NS, W), jnp.float32) ** block_scale(key_list[3], (NS, W), ((0, 512),), -0.2, 0.2)), 1.0, 8.0)
    return dict(sigma_anc=sigma_anc, structure=structure, factor=factor, diag_term=diag_term)


def reference(sigma_anc, structure, factor, diag_term):
    block_total = sigma_anc.shape[0] // B
    blocked = sigma_anc.reshape(block_total, B, block_total, B)

    def single(inputs):
        own_blocks, triangle, diag_row = inputs
        picked_rows = jnp.take(blocked, own_blocks, axis=0)
        gram_block = jnp.take(picked_rows, own_blocks, axis=2).reshape(S * B, S * B)
        product = -jnp.dot(gram_block, triangle, preferred_element_type=jnp.float32)
        variance = diag_row - jnp.sum(triangle.astype(jnp.float32) * product, axis=0)
        return product.astype(jnp.bfloat16), variance

    sigma_off, variances = lax.map(single, (structure, factor, diag_term))
    return sigma_off, variances
```

```python
import functools

import jax
import jax.numpy as jnp
from jax import lax
from jax.experimental import pallas as pl
from jax.experimental.pallas import tpu as pltpu
from jax.sharding import Mesh, PartitionSpec as P

Y, XH, Z, XL, C = 8, 2, 8, 2, 2
AXES = ("y", "xh", "z", "xl", "c")
CHIPS = ("y", "xh", "z", "xl")
PLANE = ("y", "z")
NB = 16
NU = Y * Z
S = 4
PAIRS = [(k, l) for k in range(S) for l in range(k, S)]


def rows_below(n, shape):
    return lax.broadcasted_iota(jnp.int32, shape, len(shape) - 2) < n


def deal_kernel(structure, sigma, out):
    lane = lax.broadcasted_iota(jnp.int32, (8, 128), 1)
    names = jnp.zeros((8, 128), jnp.float32)
    for k in range(S):
        names = jnp.where(lane == k, structure[0, k].astype(jnp.float32), names)
    top = rows_below(4, (8, 128))
    for u in range(NU):
        tile = sigma[pl.ds(8 * (u // 2), 8), :].astype(jnp.float32)
        if u % 2:
            tile = pltpu.roll(tile, 4, 0)
        tile = jnp.where(top, tile, names).astype(jnp.bfloat16)
        y, z = divmod(u, Z)
        for xh in range(XH):
            for xl in range(XL):
                out[((y * XH + xh) * Z + z) * XL + xl] = tile


def pick_kernel(place, names, own, other, out, slices):
    xh, xl, core = place[0], place[1], place[2]

    def merge(i, carry):
        at = pl.ds(pl.multiple_of(i * 8, 8), 8)
        mine = own[at].astype(jnp.float32)
        theirs = other[at].astype(jnp.float32)
        left = jnp.where(core == 0, mine, theirs)
        right = jnp.where(core == 0, theirs, mine)
        both = jnp.where(rows_below(4, left.shape), left, pltpu.roll(right, 4, 1))
        slices[at] = both.astype(jnp.bfloat16)
        return carry

    lax.fori_loop(0, NB * NB // 8, merge, 0)

    def pick(t, carry):
        y, z = t // Z, t % Z
        at = (((y * XH + xh) * Z + z) * XL + xl) * S
        name = [names[at + k] for k in range(S)]
        for p, (k, l) in enumerate(PAIRS):
            out[t, pl.ds(8 * p, 8), :] = slices[name[k] * NB + name[l]]
        return carry

    lax.fori_loop(0, NU, pick, 0)


def product_kernel(picked, factor, diag, off, variance, gram):
    @pl.when(pl.program_id(0) == 0)
    def _():
        for p, (k, l) in enumerate(PAIRS):
            part = picked[:, pl.ds(8 * p, 8), :].astype(jnp.float32)
            turned = pltpu.roll(part, 4, 1)
            part = part.reshape(NU // 2, 2, 8, 128)
            turned = turned.reshape(NU // 2, 2, 8, 128)
            top = rows_below(4, (NU // 2, 8, 128))
            halves = (
                jnp.where(top, part[:, 0], turned[:, 1]),
                jnp.where(top, turned[:, 0], part[:, 1]),
            )
            for h, half in enumerate(halves):
                half = half.reshape(256, 128).astype(jnp.bfloat16)
                gram[pl.ds(256 * k, 256), pl.ds(256 * l + 128 * h, 128)] = half
                if l > k:
                    gram[pl.ds(256 * l + 128 * h, 128), pl.ds(256 * k, 256)] = half.T

    minus = jnp.dot(gram[...], factor[0], preferred_element_type=jnp.float32)
    off[0] = (-minus).astype(jnp.bfloat16)
    total = jnp.sum(factor[0].astype(jnp.float32) * minus, axis=0, keepdims=True)
    variance[...] = diag[...] + total


def body(sigma, structure, factor, diag):
    width = factor.shape[2]
    tile = 256
    vmem, smem = pltpu.VMEM, pltpu.SMEM
    whole = pl.BlockSpec(memory_space=vmem)
    scalars = pl.BlockSpec(memory_space=smem)

    dealt = pl.pallas_call(
        deal_kernel,
        out_shape=jax.ShapeDtypeStruct((NB * NB, 8, 128), jnp.bfloat16),
        in_specs=[scalars, whole],
        out_specs=whole,
        name="deal",
    )(structure, sigma)
    own = lax.all_to_all(dealt, CHIPS, 0, 0, tiled=True)
    flip = [(d, d ^ 1) for d in range(2 * NB * NB)]
    other = lax.ppermute(own, AXES, flip)
    names = own[:, 4, :S].astype(jnp.int32).reshape(NB * NB * S)
    place = jnp.stack([lax.axis_index(a) for a in ("xh", "xl", "c")]).astype(jnp.int32)
    chosen = pl.pallas_call(
        pick_kernel,
        out_shape=jax.ShapeDtypeStruct((NU, 8 * len(PAIRS), 128), jnp.bfloat16),
        in_specs=[scalars, scalars, whole, whole],
        out_specs=whole,
        scratch_shapes=[vmem((NB * NB, 8, 128), jnp.bfloat16)],
        name="pick",
    )(place, names, own, other)
    picked = lax.all_to_all(chosen, PLANE, 0, 0, tiled=True)

    off, variance = pl.pallas_call(
        product_kernel,
        grid=(width // tile,),
        out_shape=(
            jax.ShapeDtypeStruct(factor.shape, jnp.bfloat16),
            jax.ShapeDtypeStruct(diag.shape, jnp.float32),
        ),
        in_specs=[
            whole,
            pl.BlockSpec((1, 1024, tile), lambda w: (0, 0, w)),
            pl.BlockSpec((1, tile), lambda w: (0, w)),
        ],
        out_specs=(
            pl.BlockSpec((1, 1024, tile), lambda w: (0, 0, w)),
            pl.BlockSpec((1, tile), lambda w: (0, w)),
        ),
        scratch_shapes=[vmem((1024, 1024), jnp.bfloat16)],
        name="product",
    )(picked, factor, diag)
    return off, variance


def solution(mesh):
    fine = Mesh(mesh.devices.reshape(Y, XH, Z, XL, C), AXES)
    return jax.shard_map(
        body,
        mesh=fine,
        in_specs=(
            P(("y", "xh"), ("z", "xl", "c")),
            P(AXES, None),
            P(AXES, None, None),
            P(AXES, None),
        ),
        out_specs=(P(AXES, None, None), P(AXES, None)),
        check_vma=False,
    )
```

```python
import jax
import jax.numpy as jnp
from jax import lax
from jax.experimental import pallas as pl
from jax.experimental.pallas import tpu as pltpu
from jax.sharding import Mesh, PartitionSpec as P

Y, XH, Z, XL, C = 8, 2, 8, 2, 2
AXES = ("y", "xh", "z", "xl", "c")
CHIPS = ("y", "xh", "z", "xl")
PLANE = ("y", "z")
NB = 16
NU = Y * Z
S = 4
PAIRS = [(k, l) for k in range(S) for l in range(k, S)]


def rows_below(n, shape):
    return lax.broadcasted_iota(jnp.int32, shape, len(shape) - 2) < n


def deal_kernel(structure, sigma, out):
    lane = lax.broadcasted_iota(jnp.int32, (8, 128), 1)
    names = jnp.zeros((8, 128), jnp.float32)
    for k in range(S):
        names = jnp.where(lane == k, structure[0, k].astype(jnp.float32), names)
    top = rows_below(4, (8, 128))
    for u in range(NU):
        tile = sigma[pl.ds(8 * (u // 2), 8), :].astype(jnp.float32)
        if u % 2:
            tile = pltpu.roll(tile, 4, 0)
        tile = jnp.where(top, tile, names).astype(jnp.bfloat16)
        y, z = divmod(u, Z)
        for xh in range(XH):
            for xl in range(XL):
                out[((y * XH + xh) * Z + z) * XL + xl] = tile


def pick_kernel(names, own, other, out, slices):
    xh, xl, core = (lax.axis_index(a) for a in ("xh", "xl", "c"))

    def merge(left, right):
        def step(i, carry):
            at = pl.ds(pl.multiple_of(i * 32, 32), 32)
            low = pltpu.roll(right[at].astype(jnp.float32), 4, 1)
            both = jnp.where(rows_below(4, low.shape), left[at].astype(jnp.float32), low)
            slices[at] = both.astype(jnp.bfloat16)
            return carry

        lax.fori_loop(0, NB * NB // 32, step, 0)

    @pl.when(core == 0)
    def _():
        merge(own, other)

    @pl.when(core != 0)
    def _():
        merge(other, own)

    def pick(y, carry):
        first = ((y * XH + xh) * Z * XL + xl) * S
        for z in range(Z):
            name = [names[first + z * XL * S + k] for k in range(S)]
            high = [n * NB for n in name]
            for p, (k, l) in enumerate(PAIRS):
                out[y * Z + z, pl.ds(8 * p, 8), :] = slices[high[k] + name[l]]
        return carry

    lax.fori_loop(0, Y, pick, 0)


def unfold(picked, p):
    part = picked[:, pl.ds(8 * p, 8), :].astype(jnp.float32)
    turned = pltpu.roll(part, 4, 1)
    part = part.reshape(NU // 2, 2, 8, 128)
    turned = turned.reshape(NU // 2, 2, 8, 128)
    top = rows_below(4, (NU // 2, 8, 128))
    left = jnp.where(top, part[:, 0], turned[:, 1])
    right = jnp.where(top, turned[:, 0], part[:, 1])
    return [h.reshape(256, 128).astype(jnp.bfloat16) for h in (left, right)]


def product_kernel(picked, factor, diag, off, variance, gram, staged, sems):
    total = diag[...]
    copies = []
    for k in range(S):
        rows = pl.ds(256 * k, 256)
        for l in range(k, S):
            for h, half in enumerate(unfold(picked, PAIRS.index((k, l)))):
                columns = pl.ds(256 * l + 128 * h, 128)
                gram[rows, columns] = half
                if l > k:
                    gram[columns, rows] = half.T
        minus = jnp.dot(gram[rows, :], factor[0], preferred_element_type=jnp.float32)
        staged[k] = (-minus).astype(jnp.bfloat16)
        copies.append(pltpu.make_async_copy(staged.at[k], off.at[0, rows], sems.at[k]))
        copies[k].start()
        total += jnp.sum(
            factor[0, rows, :].astype(jnp.float32) * minus, axis=0, keepdims=True
        )
    variance[...] = total
    for copy in copies:
        copy.wait()


def body(sigma, structure, factor, diag):
    vmem, smem = pltpu.VMEM, pltpu.SMEM
    whole = pl.BlockSpec(memory_space=vmem)
    scalars = pl.BlockSpec(memory_space=smem)

    dealt = pl.pallas_call(
        deal_kernel,
        out_shape=jax.ShapeDtypeStruct((NB * NB, 8, 128), jnp.bfloat16),
        in_specs=[scalars, whole],
        out_specs=whole,
        compiler_params=pltpu.CompilerParams(vmem_limit_bytes=2 << 20),
        name="deal",
    )(structure, sigma)
    own = lax.all_to_all(dealt, CHIPS, 0, 0, tiled=True)
    flip = [(d, d ^ 1) for d in range(2 * NB * NB)]
    other = lax.ppermute(own, AXES, flip)
    names = own[:, 4, :S].astype(jnp.int32).reshape(NB * NB * S)
    chosen = pl.pallas_call(
        pick_kernel,
        out_shape=jax.ShapeDtypeStruct((NU, 8 * len(PAIRS), 128), jnp.bfloat16),
        in_specs=[scalars, whole, whole],
        out_specs=whole,
        scratch_shapes=[vmem((NB * NB, 8, 128), jnp.bfloat16)],
        compiler_params=pltpu.CompilerParams(vmem_limit_bytes=6 << 20),
        name="pick",
    )(names, own, other)
    picked = lax.all_to_all(chosen, PLANE, 0, 0, tiled=True)

    off, variance = pl.pallas_call(
        product_kernel,
        out_shape=(
            jax.ShapeDtypeStruct(factor.shape, jnp.bfloat16),
            jax.ShapeDtypeStruct(diag.shape, jnp.float32),
        ),
        in_specs=[whole, whole, whole],
        out_specs=(pl.BlockSpec(memory_space=pl.ANY), whole),
        scratch_shapes=[
            vmem((1024, 1024), jnp.bfloat16),
            vmem((S, 256, 1024), jnp.bfloat16),
            pltpu.SemaphoreType.DMA((S,)),
        ],
        compiler_params=pltpu.CompilerParams(vmem_limit_bytes=24 << 20),
        name="product",
    )(picked, factor, diag)
    return off, variance


def solution(mesh):
    fine = Mesh(mesh.devices.reshape(Y, XH, Z, XL, C), AXES)
    return jax.shard_map(
        body,
        mesh=fine,
        in_specs=(
            P(("y", "xh"), ("z", "xl", "c")),
            P(AXES, None),
            P(AXES, None, None),
            P(AXES, None),
        ),
        out_specs=(P(AXES, None, None), P(AXES, None)),
        check_vma=False,
    )
```

```python
import jax
import jax.numpy as jnp
from jax import lax
from jax.experimental import pallas as pl
from jax.experimental.pallas import tpu as pltpu
from jax.sharding import Mesh, PartitionSpec as P

Y, XH, Z, XL, C = 8, 2, 8, 2, 2
AXES = ("y", "xh", "z", "xl", "c")
CHIPS = ("y", "xh", "z", "xl")
PLANE = ("y", "z")
NB = 16
NU = Y * Z
S = 4
PAIRS = [(k, l) for k in range(S) for l in range(k + 1, S)]
ROWS = 8 * len(PAIRS) + 4 * S


def rows_below(n, shape):
    return lax.broadcasted_iota(jnp.int32, shape, len(shape) - 2) < n


def deal_kernel(structure_hbm, sigma_hbm, dealt, structure, sigma, out, sems, out_sems):
    copies = [
        pltpu.make_async_copy(structure_hbm, structure, sems.at[0]),
        pltpu.make_async_copy(sigma_hbm, sigma, sems.at[1]),
    ]
    for copy in copies:
        copy.start()
    for copy in copies:
        copy.wait()
    lane = lax.broadcasted_iota(jnp.int32, (8, 128), 1)
    row = lax.broadcasted_iota(jnp.int32, (8, 128), 0)
    extra = jnp.zeros((8, 128), jnp.float32)
    for k in range(S):
        extra = jnp.where(lane == k, structure[0, k].astype(jnp.float32), extra)
    start = pl.multiple_of(128 * (1 - lax.axis_index("c")), 128)
    square = sigma[pl.ds(start, 128), :].astype(jnp.float32)
    on = lax.broadcasted_iota(jnp.int32, (128, 128), 0) == lax.broadcasted_iota(
        jnp.int32, (128, 128), 1
    )
    far = jnp.sum(jnp.where(on, square, 0.0), axis=0, keepdims=True)
    extra = jnp.where(row == 5, far, extra)
    for u in range(NU):
        tile = sigma[pl.ds(8 * (u // 2), 8), :].astype(jnp.float32)
        if u % 2:
            tile = pltpu.roll(tile, 4, 0)
        tile = jnp.where(row < 4, tile, extra).astype(jnp.bfloat16)
        y, z = divmod(u, Z)
        for xh in range(XH):
            for xl in range(XL):
                out[((y * XH + xh) * Z + z) * XL + xl] = tile
        if z == Z - 1:
            part = pl.ds(y * XH * Z * XL, XH * Z * XL)
            copies.append(
                pltpu.make_async_copy(out.at[part], dealt.at[part], out_sems.at[y])
            )
            copies[-1].start()
    for copy in copies[2:]:
        copy.wait()


def pick_kernel(names, own, other, out, far, slices, bands):
    y_me, xh, z_me, xl, core = (lax.axis_index(a) for a in AXES)

    def merge(left, right):
        def step(i, carry):
            at = pl.ds(pl.multiple_of(i * 32, 32), 32)
            low = pltpu.roll(right[at].astype(jnp.float32), 4, 1)
            both = jnp.where(rows_below(4, low.shape), left[at].astype(jnp.float32), low)
            slices[at] = both.astype(jnp.bfloat16)
            return carry

        lax.fori_loop(0, NB * NB // 32, step, 0)
        lane = lax.broadcasted_iota(jnp.int32, (8, 128), 1)
        i = 4 * (y_me * Z + z_me) + lax.broadcasted_iota(jnp.int32, (8, 128), 0)
        near = ((lane - i) & 255) < 128
        for r in range(NB):
            at = r * (NB + 1)
            band = jnp.where(
                near, left[at].astype(jnp.float32), right[at].astype(jnp.float32)
            )
            bands[r] = band.astype(jnp.bfloat16)

    @pl.when(core == 0)
    def _():
        merge(own, other)

    @pl.when(core != 0)
    def _():
        merge(other, own)

    mine = (((y_me * XH + xh) * Z + z_me) * XL + xl) * S
    for k in range(S):
        spare = own[names[mine + k] * (NB + 1), pl.ds(4, 4), :].astype(jnp.float32)
        far[pl.ds(k, 1), :] = spare[1:2]

    def pick(y, carry):
        first = ((y * XH + xh) * Z * XL + xl) * S
        for z in range(Z):
            t = y * Z + z
            name = [names[first + z * XL * S + k] for k in range(S)]
            high = [n * NB for n in name]
            for p, (k, l) in enumerate(PAIRS):
                out[t, pl.ds(8 * p, 8), :] = slices[high[k] + name[l]]
            for k in range(S):
                rows = pl.ds(8 * len(PAIRS) + 4 * k, 4)
                out[t, rows, :] = bands[name[k], pl.ds(0, 4), :]
        return carry

    lax.fori_loop(0, Y, pick, 0)


def unfold(picked, p):
    part = picked[:, pl.ds(8 * p, 8), :].astype(jnp.float32)
    turned = pltpu.roll(part, 4, 1)
    part = part.reshape(NU // 2, 2, 8, 128)
    turned = turned.reshape(NU // 2, 2, 8, 128)
    top = rows_below(4, (NU // 2, 8, 128))
    left = jnp.where(top, part[:, 0], turned[:, 1])
    right = jnp.where(top, turned[:, 0], part[:, 1])
    return [h.reshape(256, 128) for h in (left, right)]


def square_of(band, far):
    upper, lower = band[:128], band[128:]
    row = lax.broadcasted_iota(jnp.int32, (128, 128), 0)
    lane = lax.broadcasted_iota(jnp.int32, (128, 128), 1)
    over, under = lane > row, lane < row
    quarters = (
        (jnp.where(under, upper.T, upper), jnp.where(under, upper, lower.T)),
        (jnp.where(under, lower, upper.T), jnp.where(under, lower.T, lower)),
    )
    mixed = [jnp.where(over | under, quarters[h][1 - h], far) for h in range(2)]
    return ((quarters[0][0], mixed[0]), (mixed[1], quarters[1][1]))


def product_kernel(picked, far, factor, diag, off, variance, gram, staged, sems):
    total = diag[...]
    copies = []
    for k in range(S):
        rows = pl.ds(256 * k, 256)
        if k % 2 == 0:
            bands = unfold(picked, len(PAIRS) + k // 2)
        quarters = square_of(bands[k % 2], far[pl.ds(k, 1), :])
        for g in range(2):
            for h in range(2):
                at = (pl.ds(256 * k + 128 * g, 128), pl.ds(256 * k + 128 * h, 128))
                gram[at] = quarters[g][h].astype(jnp.bfloat16)
        for l in range(k + 1, S):
            for h, half in enumerate(unfold(picked, PAIRS.index((k, l)))):
                columns = pl.ds(256 * l + 128 * h, 128)
                half = half.astype(jnp.bfloat16)
                gram[rows, columns] = half
                gram[columns, rows] = half.T
        minus = jnp.dot(gram[rows, :], factor[0], preferred_element_type=jnp.float32)
        staged[k] = (-minus).astype(jnp.bfloat16)
        copies.append(pltpu.make_async_copy(staged.at[k], off.at[0, rows], sems.at[k]))
        copies[k].start()
        total += jnp.sum(
            factor[0, rows, :].astype(jnp.float32) * minus, axis=0, keepdims=True
        )
    variance[...] = total
    for copy in copies:
        copy.wait()


def body(sigma, structure, factor, diag):
    vmem, smem = pltpu.VMEM, pltpu.SMEM
    whole = pl.BlockSpec(memory_space=vmem)
    scalars = pl.BlockSpec(memory_space=smem)
    anywhere = pl.BlockSpec(memory_space=pl.ANY)

    dealt = pl.pallas_call(
        deal_kernel,
        out_shape=jax.ShapeDtypeStruct((NB * NB, 8, 128), jnp.bfloat16),
        in_specs=[anywhere, anywhere],
        out_specs=anywhere,
        scratch_shapes=[
            smem(structure.shape, jnp.int32),
            vmem(sigma.shape, jnp.bfloat16),
            vmem((NB * NB, 8, 128), jnp.bfloat16),
            pltpu.SemaphoreType.DMA((2,)),
            pltpu.SemaphoreType.DMA((Y,)),
        ],
        name="deal",
    )(structure, sigma)
    own = lax.all_to_all(dealt, CHIPS, 0, 0, tiled=True)
    flip = [(d, d ^ 1) for d in range(2 * NB * NB)]
    other = lax.ppermute(own, AXES, flip)
    names = own[:, 4, :S].astype(jnp.int32).reshape(NB * NB * S)
    chosen, far = pl.pallas_call(
        pick_kernel,
        out_shape=(
            jax.ShapeDtypeStruct((NU, ROWS, 128), jnp.bfloat16),
            jax.ShapeDtypeStruct((8, 128), jnp.float32),
        ),
        in_specs=[scalars, whole, whole],
        out_specs=(whole, whole),
        scratch_shapes=[
            vmem((NB * NB, 8, 128), jnp.bfloat16),
            vmem((NB, 8, 128), jnp.bfloat16),
        ],
        compiler_params=pltpu.CompilerParams(vmem_limit_bytes=6 << 20),
        name="pick",
    )(names, own, other)
    picked = lax.all_to_all(chosen, PLANE, 0, 0, tiled=True)

    off, variance = pl.pallas_call(
        product_kernel,
        out_shape=(
            jax.ShapeDtypeStruct(factor.shape, jnp.bfloat16),
            jax.ShapeDtypeStruct(diag.shape, jnp.float32),
        ),
        in_specs=[whole, whole, whole, whole],
        out_specs=(anywhere, whole),
        scratch_shapes=[
            vmem((1024, 1024), jnp.bfloat16),
            vmem((S, 256, 1024), jnp.bfloat16),
            pltpu.SemaphoreType.DMA((S,)),
        ],
        compiler_params=pltpu.CompilerParams(vmem_limit_bytes=24 << 20),
        name="product",
    )(picked, far, factor, diag)
    return off, variance


def solution(mesh):
    fine = Mesh(mesh.devices.reshape(Y, XH, Z, XL, C), AXES)
    return jax.shard_map(
        body,
        mesh=fine,
        in_specs=(
            P(("y", "xh"), ("z", "xl", "c")),
            P(AXES, None),
            P(AXES, None, None),
            P(AXES, None),
        ),
        out_specs=(P(AXES, None, None), P(AXES, None)),
        check_vma=False,
    )
```

```python
import jax
import jax.numpy as jnp
from jax import lax
from jax.experimental import pallas as pl
from jax.experimental.pallas import tpu as pltpu
from jax.sharding import Mesh, PartitionSpec as P

Y, XH, Z, XL, C = 8, 2, 8, 2, 2
AXES = ("y", "xh", "z", "xl", "c")
CHIPS = ("y", "xh", "z", "xl")
PLANE = ("y", "z")
NB = 16
NU = Y * Z
S = 4
PAIRS = [(k, l) for k in range(S) for l in range(k + 1, S)]
ROWS = 8 * len(PAIRS) + 4 * S


def iota(shape, dim):
    return lax.broadcasted_iota(jnp.int32, shape, dim)


def apart(shape):
    return (iota(shape, len(shape) - 1) - iota(shape, len(shape) - 2)) & 127


def kept(distance, low):
    return ((distance - low) & 127) < 64


def deal_kernel(structure_hbm, sigma_hbm, dealt, structure, sigma, out, sems, out_sems):
    copies = [
        pltpu.make_async_copy(structure_hbm, structure, sems.at[0]),
        pltpu.make_async_copy(sigma_hbm, sigma, sems.at[1]),
    ]
    for copy in copies:
        copy.start()
    for copy in copies:
        copy.wait()
    y_me, xh_me, z_me, xl_me, core = (lax.axis_index(a) for a in AXES)
    r, b = y_me * XH + xh_me, z_me * XL + xl_me
    lane, row = iota((8, 128), 1), iota((8, 128), 0)
    extra = jnp.zeros((8, 128), jnp.float32)
    for k in range(S):
        extra = jnp.where(lane == k, structure[0, k].astype(jnp.float32), extra)
    start = pl.multiple_of(128 * core, 128)
    square = sigma[pl.ds(start, 128), :].astype(jnp.float32)
    far = jnp.where(apart((128, 128)) == 64, square, 0.0)
    extra = jnp.where(row == 3, jnp.sum(far, axis=0, keepdims=True), extra)
    first = (lane < 64) == (core == 0)
    for v in range(NU // 2):
        tile = sigma[pl.ds(8 * v, 8), :].astype(jnp.float32)
        low = jnp.where(r == b, (v // 16 > core).astype(jnp.int32), (r > b).astype(jnp.int32))
        keep = kept(lane - row - 8 * v, low)
        tile = jnp.where(keep, tile, pltpu.roll(tile, 64, 1))
        tile = jnp.where(first, tile, pltpu.roll(tile, 6, 0))
        for odd in range(2):
            part = pltpu.roll(tile, 4, 0) if odd else tile
            part = jnp.where(row < 2, part, extra)[:4].astype(jnp.bfloat16)
            y, z = divmod(2 * v + odd, Z)
            for xh in range(XH):
                for xl in range(XL):
                    out[((y * XH + xh) * Z + z) * XL + xl] = part
        if z == Z - 1:
            part = pl.ds(y * XH * Z * XL, XH * Z * XL)
            copies.append(
                pltpu.make_async_copy(out.at[part], dealt.at[part], out_sems.at[y])
            )
            copies[-1].start()
    for copy in copies[2:]:
        copy.wait()


def pick_kernel(names, own, other, out, far, slices):
    y_me, xh, z_me, xl, core = (lax.axis_index(a) for a in AXES)
    mine = (((y_me * XH + xh) * Z + z_me) * XL + xl) * S

    def merge(left, right):
        def step(r, carry):
            parts = []
            for at in ((r, slice(None)), (slice(None), r)):
                one = left[at][:, :2].astype(jnp.float32)
                two = right[at][:, :2].astype(jnp.float32)
                west = iota(one.shape, 2) < 64
                parts += [jnp.where(west, one, two), jnp.where(west, two, one)]
            slices[r] = jnp.concatenate(parts, axis=1).astype(jnp.bfloat16)
            return carry

        lax.fori_loop(0, NB, step, 0)
        for k in range(S):
            at = names[mine + k]
            for g, half in enumerate((left, right)):
                far[4 * g + k : 4 * g + k + 1, :] = half[at, at].astype(jnp.float32)[3:4]

    @pl.when(core == 0)
    def _():
        merge(own, other)

    @pl.when(core != 0)
    def _():
        merge(other, own)

    def pick(y, carry):
        first = ((y * XH + xh) * Z * XL + xl) * S
        for z in range(Z):
            name = [names[first + z * XL * S + k] for k in range(S)]
            for p, (k, l) in enumerate(PAIRS):
                out[y * Z + z, pl.ds(8 * p, 8), :] = slices[name[k], name[l]]
            for k in range(S):
                rows = pl.ds(8 * len(PAIRS) + 4 * k, 4)
                out[y * Z + z, rows, :] = slices[name[k], name[k], pl.ds(0, 4), :]
        return carry

    lax.fori_loop(0, Y, pick, 0)


def unfold(picked, p):
    part = picked[:, pl.ds(8 * p, 8), :].astype(jnp.float32)
    turned = pltpu.roll(part, 4, 1)
    part = part.reshape(NU // 2, 2, 8, 128)
    turned = turned.reshape(NU // 2, 2, 8, 128)
    top = iota((NU // 2, 8, 128), 1) < 4
    first = (iota((256, 128), 1) < 64) == (iota((256, 128), 0) % 4 < 2)
    result = []
    for half in (
        jnp.where(top, part[:, 0], turned[:, 1]),
        jnp.where(top, turned[:, 0], part[:, 1]),
    ):
        half = half.reshape(256, 128)
        swapped = pltpu.roll(half, 64, 1).astype(jnp.bfloat16)
        half = half.astype(jnp.bfloat16)
        result.append((jnp.where(first, half, swapped), jnp.where(first, swapped, half)))
    return result


def quarter(half, g, h):
    return half[h][128 * g : 128 * g + 128]


def product_kernel(
    structure, picked, far, factor, diag, off, variance, gram, staged, sems
):
    total = diag[...]
    copies = []
    gap = apart((128, 128))
    for k in range(S):
        rows = pl.ds(256 * k, 256)
        for l in range(k, S):
            if l == k:
                if k % 2 == 0:
                    pair = unfold(picked, len(PAIRS) + k // 2)
                one = two = pair[k % 2]
            else:
                one, two = unfold(picked, PAIRS.index((k, l)))
                low = (structure[0, k] > structure[0, l]).astype(jnp.int32)
            for g in range(2):
                for h in range(2):
                    keep = kept(gap, int(g > h) if l == k else low)
                    value = jnp.where(keep, quarter(one, g, h), quarter(two, h, g).T)
                    if l == k and g == h:
                        spare = jnp.broadcast_to(far[pl.ds(4 * g + k, 1), :], value.shape)
                        value = jnp.where(gap == 64, spare.astype(jnp.bfloat16), value)
                    down, across = pl.ds(256 * k + 128 * g, 128), pl.ds(256 * l + 128 * h, 128)
                    gram[down, across] = value
                    if l > k:
                        gram[across, down] = value.T
        minus = jnp.dot(gram[rows, :], factor[0], preferred_element_type=jnp.float32)
        staged[k] = (-minus).astype(jnp.bfloat16)
        copies.append(pltpu.make_async_copy(staged.at[k], off.at[0, rows], sems.at[k]))
        copies[k].start()
        total += jnp.sum(
            factor[0, rows, :].astype(jnp.float32) * minus, axis=0, keepdims=True
        )
    variance[...] = total
    for copy in copies:
        copy.wait()


def body(sigma, structure, factor, diag):
    vmem, smem = pltpu.VMEM, pltpu.SMEM
    whole = pl.BlockSpec(memory_space=vmem)
    scalars = pl.BlockSpec(memory_space=smem)
    anywhere = pl.BlockSpec(memory_space=pl.ANY)

    dealt = pl.pallas_call(
        deal_kernel,
        out_shape=jax.ShapeDtypeStruct((NB * NB, 4, 128), jnp.bfloat16),
        in_specs=[anywhere, anywhere],
        out_specs=anywhere,
        scratch_shapes=[
            smem(structure.shape, jnp.int32),
            vmem(sigma.shape, jnp.bfloat16),
            vmem((NB * NB, 4, 128), jnp.bfloat16),
            pltpu.SemaphoreType.DMA((2,)),
            pltpu.SemaphoreType.DMA((Y,)),
        ],
        name="deal",
    )(structure, sigma)
    own = lax.all_to_all(dealt, CHIPS, 0, 0, tiled=True)
    flip = [(d, d ^ 1) for d in range(2 * NB * NB)]
    other = lax.ppermute(own, AXES, flip)
    grid = (NB, NB, 4, 128)
    names = own[:, 2, :S].astype(jnp.int32).reshape(NB * NB * S)
    chosen, far = pl.pallas_call(
        pick_kernel,
        out_shape=(
            jax.ShapeDtypeStruct((NU, ROWS, 128), jnp.bfloat16),
            jax.ShapeDtypeStruct((8, 128), jnp.float32),
        ),
        in_specs=[scalars, whole, whole],
        out_specs=(whole, whole),
        scratch_shapes=[vmem((NB, NB, 8, 128), jnp.bfloat16)],
        compiler_params=pltpu.CompilerParams(vmem_limit_bytes=6 << 20),
        name="pick",
    )(names, own.reshape(grid), other.reshape(grid))
    picked = lax.all_to_all(chosen, PLANE, 0, 0, tiled=True)

    off, variance = pl.pallas_call(
        product_kernel,
        out_shape=(
            jax.ShapeDtypeStruct(factor.shape, jnp.bfloat16),
            jax.ShapeDtypeStruct(diag.shape, jnp.float32),
        ),
        in_specs=[scalars, whole, whole, whole, whole],
        out_specs=(anywhere, whole),
        scratch_shapes=[
            vmem((1024, 1024), jnp.bfloat16),
            vmem((S, 256, 1024), jnp.bfloat16),
            pltpu.SemaphoreType.DMA((S,)),
        ],
        compiler_params=pltpu.CompilerParams(vmem_limit_bytes=24 << 20),
        name="product",
    )(structure, picked, far, factor, diag)
    return off, variance


def solution(mesh):
    fine = Mesh(mesh.devices.reshape(Y, XH, Z, XL, C), AXES)
    return jax.shard_map(
        body,
        mesh=fine,
        in_specs=(
            P(("y", "xh"), ("z", "xl", "c")),
            P(AXES, None),
            P(AXES, None, None),
            P(AXES, None),
        ),
        out_specs=(P(AXES, None, None), P(AXES, None)),
        check_vma=False,
    )
```

```python
import jax
import jax.numpy as jnp
from jax import lax
from jax.experimental import pallas as pl
from jax.experimental.pallas import tpu as pltpu
from jax.sharding import Mesh, PartitionSpec as P

SIZES = dict(yh=4, yl=2, xh=2, zh=4, zl=2, xl=2, c=2)
AXES = tuple(SIZES)
CHIPS = AXES[:-1]
NEAR = ("yl", "xh", "zl", "xl")
NB = 16
NU = 16
S = 4
PAIRS = [(k, l) for k in range(S) for l in range(k + 1, S)]
ORDER = [q for k, l in PAIRS for q in ((k, l), (l, k))] + [(k, k) for k in range(S)]


def iota(shape, dim):
    return lax.broadcasted_iota(jnp.int32, shape, dim)


def apart(shape):
    return (iota(shape, len(shape) - 1) - iota(shape, len(shape) - 2)) & 127


def kept(distance, low):
    return ((distance - low) & 127) < 64


def place():
    yh, yl, xh, zh, zl, xl, core = (lax.axis_index(a) for a in AXES)
    return 4 * yh + 2 * yl + xh, 4 * zh + 2 * zl + xl, core


def deal_kernel(structure_hbm, sigma_hbm, dealt, structure, sigma, out, sems, out_sems):
    copies = [
        pltpu.make_async_copy(structure_hbm, structure, sems.at[0]),
        pltpu.make_async_copy(sigma_hbm, sigma, sems.at[1]),
    ]
    for copy in copies:
        copy.start()
    for copy in copies:
        copy.wait()
    r, b, core = place()
    lane, row = iota((8, 128), 1), iota((8, 128), 0)
    extra = jnp.zeros((8, 128), jnp.float32)
    for k in range(S):
        extra = jnp.where(lane == k, structure[0, k].astype(jnp.float32), extra)
    start = pl.multiple_of(128 * core, 128)
    square = sigma[pl.ds(start, 128), :].astype(jnp.float32)
    far = jnp.where(apart((128, 128)) == 64, square, 0.0)
    extra = jnp.where(row == 1, jnp.sum(far, axis=0, keepdims=True), extra)
    extra = extra[:2].astype(jnp.bfloat16)
    first = (lane < 64) == (core == 0)
    for u in range(NU):
        low = jnp.where(r == b, (u // 8 > core).astype(jnp.int32), (r > b).astype(jnp.int32))
        tiles = []
        for v in (2 * u, 2 * u + 1):
            tile = sigma[pl.ds(8 * v, 8), :].astype(jnp.float32)
            keep = kept(lane - row - 8 * v, low)
            tiles.append(jnp.where(keep, tile, pltpu.roll(tile, 64, 1)))
        tile = jnp.where(first, *tiles)
        for j in range(4):
            out[u // 4, u % 4, j] = tile[2 * j : 2 * j + 2].astype(jnp.bfloat16)
        out[u // 4, u % 4, 4] = extra
    spread = [
        pltpu.make_async_copy(out, dealt.at[yh, :, zh], out_sems.at[yh, zh])
        for yh in range(4)
        for zh in range(4)
    ]
    for copy in spread:
        copy.start()
    for copy in spread:
        copy.wait()


def pick_kernel(names, own, other, out, far):
    r_me, b_me, core = place()
    y0, z0 = r_me // 4 * 4, b_me // 4 * 4
    west = iota((8, 128), 1) < 64

    def run(left, right):
        mine = (r_me * NB + b_me) * S
        for k in range(S):
            at = names[mine + k]
            for g, half in enumerate((left, right)):
                far[4 * g + k : 4 * g + k + 1, :] = half[at, at, 4].astype(jnp.float32)[1:2]

        def step(t, carry):
            first = ((y0 + t // 4) * NB + z0 + t % 4) * S
            name = [names[first + k] for k in range(S)]
            for q, (k, l) in enumerate(ORDER):
                at = (name[k], name[l], pl.ds(0, 4))
                one = left[at].astype(jnp.float32).reshape(8, 128)
                two = right[at].astype(jnp.float32).reshape(8, 128)
                both = [jnp.where(west, one, two), jnp.where(west, two, one)]
                rows = pl.ds(16 * q, 16)
                out[t, rows, :] = jnp.concatenate(both, axis=0).astype(jnp.bfloat16)
            return carry

        lax.fori_loop(0, NU, step, 0)

    @pl.when(core == 0)
    def _():
        run(own, other)

    @pl.when(core != 0)
    def _():
        run(other, own)


def unfold(picked, q):
    half = picked[:, pl.ds(16 * q, 16), :].reshape(256, 128)
    swapped = pltpu.roll(half.astype(jnp.float32), 64, 1).astype(jnp.bfloat16)
    first = (iota((256, 128), 1) < 64) == (iota((256, 128), 0) % 16 < 8)
    return jnp.where(first, half, swapped), jnp.where(first, swapped, half)


def quarter(half, g, h):
    return half[h][128 * g : 128 * g + 128]


def product_kernel(
    structure, picked, far, factor, diag, off, variance, gram, staged, sems
):
    total = diag[...]
    copies = []
    gap = apart((128, 128))
    for k in range(S):
        rows = pl.ds(256 * k, 256)
        for l in range(k, S):
            if l == k:
                one = two = unfold(picked, ORDER.index((k, k)))
            else:
                one = unfold(picked, ORDER.index((k, l)))
                two = unfold(picked, ORDER.index((l, k)))
                low = (structure[0, k] > structure[0, l]).astype(jnp.int32)
            for g in range(2):
                for h in range(2):
                    keep = kept(gap, int(g > h) if l == k else low)
                    value = jnp.where(keep, quarter(one, g, h), quarter(two, h, g).T)
                    if l == k and g == h:
                        spare = jnp.broadcast_to(far[pl.ds(4 * g + k, 1), :], value.shape)
                        value = jnp.where(gap == 64, spare.astype(jnp.bfloat16), value)
                    down, across = pl.ds(256 * k + 128 * g, 128), pl.ds(256 * l + 128 * h, 128)
                    gram[down, across] = value
                    if l > k:
                        gram[across, down] = value.T
        minus = jnp.dot(gram[rows, :], factor[0], preferred_element_type=jnp.float32)
        staged[k] = (-minus).astype(jnp.bfloat16)
        copies.append(pltpu.make_async_copy(staged.at[k], off.at[0, rows], sems.at[k]))
        copies[k].start()
        total += jnp.sum(
            factor[0, rows, :].astype(jnp.float32) * minus, axis=0, keepdims=True
        )
    variance[...] = total
    for copy in copies:
        copy.wait()


def body(sigma, structure, factor, diag):
    vmem, smem = pltpu.VMEM, pltpu.SMEM
    whole = pl.BlockSpec(memory_space=vmem)
    scalars = pl.BlockSpec(memory_space=smem)
    anywhere = pl.BlockSpec(memory_space=pl.ANY)

    message = (5, 2, 128)
    dealt = pl.pallas_call(
        deal_kernel,
        out_shape=jax.ShapeDtypeStruct((4, 4, 4, 4) + message, jnp.bfloat16),
        in_specs=[anywhere, anywhere],
        out_specs=anywhere,
        scratch_shapes=[
            smem(structure.shape, jnp.int32),
            vmem(sigma.shape, jnp.bfloat16),
            vmem((4, 4) + message, jnp.bfloat16),
            pltpu.SemaphoreType.DMA((2,)),
            pltpu.SemaphoreType.DMA((4, 4)),
        ],
        name="deal",
    )(structure, sigma)
    own = lax.all_to_all(dealt.reshape((NB * NB,) + message), CHIPS, 0, 0, tiled=True)
    flip = [(d, d ^ 1) for d in range(2 * NB * NB)]
    other = lax.ppermute(own, AXES, flip)
    grid = (NB, NB) + message
    names = own[:, 4, 0, :S].astype(jnp.int32).reshape(NB * NB * S)
    chosen, far = pl.pallas_call(
        pick_kernel,
        out_shape=(
            jax.ShapeDtypeStruct((NU, 16 * len(ORDER), 128), jnp.bfloat16),
            jax.ShapeDtypeStruct((8, 128), jnp.float32),
        ),
        in_specs=[scalars, whole, whole],
        out_specs=(whole, whole),
        compiler_params=pltpu.CompilerParams(vmem_limit_bytes=6 << 20),
        name="pick",
    )(names, own.reshape(grid), other.reshape(grid))
    picked = lax.all_to_all(chosen, NEAR, 0, 0, tiled=True)

    off, variance = pl.pallas_call(
        product_kernel,
        out_shape=(
            jax.ShapeDtypeStruct(factor.shape, jnp.bfloat16),
            jax.ShapeDtypeStruct(diag.shape, jnp.float32),
        ),
        in_specs=[scalars, whole, whole, whole, whole],
        out_specs=(anywhere, whole),
        scratch_shapes=[
            vmem((1024, 1024), jnp.bfloat16),
            vmem((S, 256, 1024), jnp.bfloat16),
            pltpu.SemaphoreType.DMA((S,)),
        ],
        compiler_params=pltpu.CompilerParams(vmem_limit_bytes=24 << 20),
        name="product",
    )(structure, picked, far, factor, diag)
    return off, variance


def solution(mesh):
    fine = Mesh(mesh.devices.reshape(tuple(SIZES.values())), AXES)
    return jax.shard_map(
        body,
        mesh=fine,
        in_specs=(
            P(AXES[:3], AXES[3:]),
            P(AXES, None),
            P(AXES, None, None),
            P(AXES, None),
        ),
        out_specs=(P(AXES, None, None), P(AXES, None)),
        check_vma=False,
    )
```

```python
import jax
import jax.numpy as jnp
from jax import lax
from jax.experimental import pallas as pl
from jax.experimental.pallas import tpu as pltpu
from jax.sharding import Mesh, PartitionSpec as P

SIZES = dict(yh=4, yl=2, xh=2, zh=4, zl=2, xl=2, c=2)
AXES = tuple(SIZES)
CHIPS = AXES[:-1]
NEAR = ("yl", "xh", "zl", "xl")
NB = 16
NU = 16
S = 4
ENDS, RUNS = (1, 4), (1, 2)
PAIRS = [(k, l) for k in range(S) for l in range(k + 1, S)]
ORDER = [q for k, l in PAIRS for q in ((k, l), (l, k))] + [(k, k) for k in range(S)]


def iota(shape, dim):
    return lax.broadcasted_iota(jnp.int32, shape, dim)


def apart(shape):
    return (iota(shape, len(shape) - 1) - iota(shape, len(shape) - 2)) & 127


def kept(distance, low):
    return ((distance - low) & 127) < 64


def place():
    yh, yl, xh, zh, zl, xl, core = (lax.axis_index(a) for a in AXES)
    return 4 * yh + 2 * yl + xh, 4 * zh + 2 * zl + xl, core


def deal_kernel(structure_hbm, sigma_hbm, dealt, structure, sigma, out, sems, out_sems):
    copies = [
        pltpu.make_async_copy(structure_hbm, structure, sems.at[0]),
        pltpu.make_async_copy(sigma_hbm, sigma, sems.at[1]),
    ]
    for copy in copies:
        copy.start()
    for copy in copies:
        copy.wait()
    r, b, core = place()
    lane, row = iota((8, 128), 1), iota((8, 128), 0)
    extra = jnp.zeros((8, 128), jnp.float32)
    for k in range(S):
        extra = jnp.where(lane == k, structure[0, k].astype(jnp.float32), extra)
    start = pl.multiple_of(128 * core, 128)
    square = -sigma[pl.ds(start, 128), :].astype(jnp.float32)
    far = jnp.where(apart((128, 128)) == 64, square, 0.0)
    extra = jnp.where(row == 1, jnp.sum(far, axis=0, keepdims=True), extra)
    extra = extra[:2].astype(jnp.bfloat16)
    first = (lane < 64) == (core == 0)
    for u in range(NU):
        low = jnp.where(r == b, (u // 8 > core).astype(jnp.int32), (r > b).astype(jnp.int32))
        tiles = []
        for v in (2 * u, 2 * u + 1):
            tile = -sigma[pl.ds(8 * v, 8), :].astype(jnp.float32)
            keep = kept(lane - row - 8 * v, low)
            tiles.append(jnp.where(keep, tile, pltpu.roll(tile, 64, 1)))
        tile = jnp.where(first, *tiles)
        for j in range(4):
            out[u // 4, u % 4, j] = tile[2 * j : 2 * j + 2].astype(jnp.bfloat16)
        out[u // 4, u % 4, 4] = extra
    spread = [
        pltpu.make_async_copy(out, dealt.at[yh, :, zh], out_sems.at[yh, zh])
        for yh in range(4)
        for zh in range(4)
    ]
    for copy in spread:
        copy.start()
    for copy in spread:
        copy.wait()


def pick_kernel(names, own, other, out, far):
    r_me, b_me, core = place()
    y0, z0 = r_me // 4 * 4, b_me // 4 * 4
    west = iota((8, 128), 1) < 64

    def run(left, right):
        mine = (r_me * NB + b_me) * S
        for k in range(S):
            at = names[mine + k]
            for g, half in enumerate((left, right)):
                far[4 * g + k : 4 * g + k + 1, :] = half[at, at, 4].astype(jnp.float32)[1:2]

        def step(i, carry):
            for j in range(4):
                t = 4 * i + j
                first = ((y0 + i) * NB + z0 + j) * S
                name = [names[first + k] for k in range(S)]
                for q, (k, l) in enumerate(ORDER):
                    at = (name[k], name[l], pl.ds(0, 4))
                    one = left[at].astype(jnp.float32).reshape(8, 128)
                    two = right[at].astype(jnp.float32).reshape(8, 128)
                    both = [jnp.where(west, one, two), jnp.where(west, two, one)]
                    rows = pl.ds(16 * q, 16)
                    out[t, rows, :] = jnp.concatenate(both, axis=0).astype(jnp.bfloat16)
            return carry

        lax.fori_loop(0, NU // 4, step, 0)

    @pl.when(core == 0)
    def _():
        run(own, other)

    @pl.when(core != 0)
    def _():
        run(other, own)


def unfold(picked, q):
    half = picked[:, pl.ds(16 * q, 16), :].reshape(256, 128)
    swapped = pltpu.roll(half.astype(jnp.float32), 64, 1).astype(jnp.bfloat16)
    first = (iota((256, 128), 1) < 64) == (iota((256, 128), 0) % 16 < 8)
    return jnp.where(first, half, swapped), jnp.where(first, swapped, half)


def quarter(half, g, h):
    return half[h][128 * g : 128 * g + 128]


def product_kernel(
    structure, picked, far, factor, diag, off, variance, gram, staged, sems
):
    copies = []
    gap = apart((128, 128))
    for k in range(S):
        rows = pl.ds(256 * k, 256)
        for l in range(k, S):
            if l == k:
                one = two = unfold(picked, ORDER.index((k, k)))
            else:
                one = unfold(picked, ORDER.index((k, l)))
                two = unfold(picked, ORDER.index((l, k)))
                low = (structure[0, k] > structure[0, l]).astype(jnp.int32)
            for g in range(2):
                for h in range(2):
                    keep = kept(gap, int(g > h) if l == k else low)
                    value = jnp.where(keep, quarter(one, g, h), quarter(two, h, g).T)
                    if l == k and g == h:
                        spare = jnp.broadcast_to(far[pl.ds(4 * g + k, 1), :], value.shape)
                        value = jnp.where(gap == 64, spare.astype(jnp.bfloat16), value)
                    down, across = pl.ds(256 * k + 128 * g, 128), pl.ds(256 * l + 128 * h, 128)
                    gram[down, across] = value
                    if l > k:
                        gram[across, down] = value.T
        if k + 1 not in ENDS:
            continue
        start = max((end for end in ENDS if end <= k), default=0)
        rows = pl.ds(256 * start, 256 * (k + 1 - start))
        runs = RUNS[ENDS.index(k + 1)]
        for run in range(runs):
            columns = pl.ds(1024 // runs * run, 1024 // runs)
            part = factor[0, :, columns]
            product = jnp.dot(gram[rows, :], part, preferred_element_type=jnp.float32)
            staged[rows, columns] = product.astype(jnp.bfloat16)
            copies.append(
                pltpu.make_async_copy(
                    staged.at[rows, columns], off.at[0, rows, columns], sems.at[len(copies)]
                )
            )
            copies[-1].start()
            mine = factor[0, rows, columns].astype(jnp.float32)
            total = jnp.sum(mine * product, axis=0, keepdims=True)
            variance[:, columns] = (diag if start == 0 else variance)[:, columns] - total
    for copy in copies:
        copy.wait()


def body(sigma, structure, factor, diag):
    vmem, smem = pltpu.VMEM, pltpu.SMEM
    whole = pl.BlockSpec(memory_space=vmem)
    scalars = pl.BlockSpec(memory_space=smem)
    anywhere = pl.BlockSpec(memory_space=pl.ANY)

    message = (5, 2, 128)
    dealt = pl.pallas_call(
        deal_kernel,
        out_shape=jax.ShapeDtypeStruct((4, 4, 4, 4) + message, jnp.bfloat16),
        in_specs=[anywhere, anywhere],
        out_specs=anywhere,
        scratch_shapes=[
            smem(structure.shape, jnp.int32),
            vmem(sigma.shape, jnp.bfloat16),
            vmem((4, 4) + message, jnp.bfloat16),
            pltpu.SemaphoreType.DMA((2,)),
            pltpu.SemaphoreType.DMA((4, 4)),
        ],
        name="deal",
    )(structure, sigma)
    own = lax.all_to_all(dealt.reshape((NB * NB,) + message), CHIPS, 0, 0, tiled=True)
    flip = [(d, d ^ 1) for d in range(2 * NB * NB)]
    other = lax.ppermute(own, AXES, flip)
    grid = (NB, NB) + message
    names = own[:, 4, 0, :S].astype(jnp.int32).reshape(NB * NB * S)
    chosen, far = pl.pallas_call(
        pick_kernel,
        out_shape=(
            jax.ShapeDtypeStruct((NU, 16 * len(ORDER), 128), jnp.bfloat16),
            jax.ShapeDtypeStruct((8, 128), jnp.float32),
        ),
        in_specs=[scalars, whole, whole],
        out_specs=(whole, whole),
        compiler_params=pltpu.CompilerParams(vmem_limit_bytes=6 << 20),
        name="pick",
    )(names, own.reshape(grid), other.reshape(grid))
    picked = lax.all_to_all(chosen, NEAR, 0, 0, tiled=True)

    off, variance = pl.pallas_call(
        product_kernel,
        out_shape=(
            jax.ShapeDtypeStruct(factor.shape, jnp.bfloat16),
            jax.ShapeDtypeStruct(diag.shape, jnp.float32),
        ),
        in_specs=[scalars, whole, whole, whole, whole],
        out_specs=(anywhere, whole),
        scratch_shapes=[
            vmem((1024, 1024), jnp.bfloat16),
            vmem((1024, 1024), jnp.bfloat16),
            pltpu.SemaphoreType.DMA((sum(RUNS),)),
        ],
        compiler_params=pltpu.CompilerParams(vmem_limit_bytes=24 << 20),
        name="product",
    )(structure, picked, far, factor, diag)
    return off, variance


def solution(mesh):
    fine = Mesh(mesh.devices.reshape(tuple(SIZES.values())), AXES)
    return jax.shard_map(
        body,
        mesh=fine,
        in_specs=(
            P(AXES[:3], AXES[3:]),
            P(AXES, None),
            P(AXES, None, None),
            P(AXES, None),
        ),
        out_specs=(P(AXES, None, None), P(AXES, None)),
        check_vma=False,
    )
```

```python
import jax
import jax.numpy as jnp
from jax import lax
from jax.experimental import pallas as pl
from jax.experimental.pallas import tpu as pltpu
from jax.sharding import Mesh, PartitionSpec as P

SIZES = dict(yh=4, yl=2, xh=2, zh=4, zl=2, xl=2, c=2)
AXES = tuple(SIZES)
NEAR = ("yl", "zl", "xh", "xl")
CHIPS = ("yh", "zh") + NEAR
NB = 16
NU = 16
S = 4
PAIRS = [(k, l) for k in range(S) for l in range(k + 1, S)]
ORDER = [q for k, l in PAIRS for q in ((k, l), (l, k))] + [(k, k) for k in range(S)]


def iota(shape, dim):
    return lax.broadcasted_iota(jnp.int32, shape, dim)


def apart(shape):
    return (iota(shape, len(shape) - 1) - iota(shape, len(shape) - 2)) & 127


def kept(distance, low):
    return ((distance - low) & 127) < 64


def place():
    yh, yl, xh, zh, zl, xl, core = (lax.axis_index(a) for a in AXES)
    near = 8 * yl + 4 * zl + 2 * xh + xl
    return 4 * yh + 2 * yl + xh, 4 * zh + 2 * zl + xl, core, 4 * yh + zh, near


def shares(n):
    high, middle, low = n >> 2, (n >> 1) & 1, n & 1
    return 64 * high + 8 * middle + 2 * low, 16 * high + 4 * middle + low


def deal_kernel(structure_hbm, sigma_hbm, dealt, structure, sigma, out, sems, out_sems):
    copies = [
        pltpu.make_async_copy(structure_hbm, structure, sems.at[0]),
        pltpu.make_async_copy(sigma_hbm, sigma, sems.at[1]),
    ]
    for copy in copies:
        copy.start()
    for copy in copies:
        copy.wait()
    r, b, core, _, _ = place()
    lane, row = iota((8, 128), 1), iota((8, 128), 0)
    extra = jnp.zeros((8, 128), jnp.float32)
    for k in range(S):
        for h, share in enumerate(shares(structure[0, k])):
            extra = jnp.where(lane == S * h + k, share.astype(jnp.float32), extra)
    start = pl.multiple_of(128 * core, 128)
    square = -sigma[pl.ds(start, 128), :].astype(jnp.float32)
    far = jnp.where(apart((128, 128)) == 64, square, 0.0)
    extra = jnp.where(row == 1, jnp.sum(far, axis=0, keepdims=True), extra)
    extra = extra[:2].astype(jnp.bfloat16)
    first = (lane < 64) == (core == 0)
    for u in range(NU):
        low = jnp.where(r == b, (u // 8 > core).astype(jnp.int32), (r > b).astype(jnp.int32))
        tiles = []
        for v in (2 * u, 2 * u + 1):
            tile = -sigma[pl.ds(8 * v, 8), :].astype(jnp.float32)
            keep = kept(lane - row - 8 * v, low)
            tiles.append(jnp.where(keep, tile, pltpu.roll(tile, 64, 1)))
        tile = jnp.where(first, *tiles)
        for j in range(4):
            out[u, j] = tile[2 * j : 2 * j + 2].astype(jnp.bfloat16)
        out[u, 4] = extra
    spread = [
        pltpu.make_async_copy(out, dealt.at[yh, zh], out_sems.at[yh, zh])
        for yh in range(4)
        for zh in range(4)
    ]
    for copy in spread:
        copy.start()
    for copy in spread:
        copy.wait()


def pick_kernel(names, own, other, out, far):
    _, _, core, box, near = place()
    west = iota((8, 128), 1) < 64

    def run(left, right):
        mine = (box * NU + near) * 2 * S
        for k in range(S):
            at = names[mine + k] + names[mine + S + k]
            for g, half in enumerate((left, right)):
                far[4 * g + k : 4 * g + k + 1, :] = half[at, 4].astype(jnp.float32)[1:2]

        def step(i, carry):
            for t in range(4):
                t = 4 * i + t
                first = (box * NU + t) * 2 * S
                name = [names[first + k] for k in range(2 * S)]
                for q, (k, l) in enumerate(ORDER):
                    at = (name[k] + name[S + l], pl.ds(0, 4))
                    one = left[at].astype(jnp.float32).reshape(8, 128)
                    two = right[at].astype(jnp.float32).reshape(8, 128)
                    both = [jnp.where(west, one, two), jnp.where(west, two, one)]
                    rows = pl.ds(16 * q, 16)
                    out[t, rows, :] = jnp.concatenate(both, axis=0).astype(jnp.bfloat16)
            return carry

        lax.fori_loop(0, NU // 4, step, 0)

    @pl.when(core == 0)
    def _():
        run(own, other)

    @pl.when(core != 0)
    def _():
        run(other, own)


def unfold(picked, q):
    half = picked[:, pl.ds(16 * q, 16), :].reshape(256, 128)
    swapped = pltpu.roll(half.astype(jnp.float32), 64, 1).astype(jnp.bfloat16)
    first = (iota((256, 128), 1) < 64) == (iota((256, 128), 0) % 16 < 8)
    return jnp.where(first, half, swapped), jnp.where(first, swapped, half)


def quarter(half, g, h):
    return half[h][128 * g : 128 * g + 128]


def product_kernel(
    structure, picked, far, factor, diag, off, variance, gram, staged, sems
):
    total = diag[...]
    copies = []
    gap = apart((128, 128))
    for k in range(S):
        rows = pl.ds(256 * k, 256)
        for l in range(k, S):
            if l == k:
                one = two = unfold(picked, ORDER.index((k, k)))
            else:
                one = unfold(picked, ORDER.index((k, l)))
                two = unfold(picked, ORDER.index((l, k)))
                low = (structure[0, k] > structure[0, l]).astype(jnp.int32)
            for g in range(2):
                for h in range(2):
                    keep = kept(gap, int(g > h) if l == k else low)
                    value = jnp.where(keep, quarter(one, g, h), quarter(two, h, g).T)
                    if l == k and g == h:
                        spare = jnp.broadcast_to(far[pl.ds(4 * g + k, 1), :], value.shape)
                        value = jnp.where(gap == 64, spare.astype(jnp.bfloat16), value)
                    down, across = pl.ds(256 * k + 128 * g, 128), pl.ds(256 * l + 128 * h, 128)
                    gram[down, across] = value
                    if l > k:
                        gram[across, down] = value.T
        product = jnp.dot(gram[rows, :], factor[0], preferred_element_type=jnp.float32)
        staged[k] = product.astype(jnp.bfloat16)
        copies.append(pltpu.make_async_copy(staged.at[k], off.at[0, rows], sems.at[k]))
        copies[k].start()
        total -= jnp.sum(
            factor[0, rows, :].astype(jnp.float32) * product, axis=0, keepdims=True
        )
    variance[...] = total
    for copy in copies:
        copy.wait()


def body(sigma, structure, factor, diag):
    vmem, smem = pltpu.VMEM, pltpu.SMEM
    whole = pl.BlockSpec(memory_space=vmem)
    scalars = pl.BlockSpec(memory_space=smem)
    anywhere = pl.BlockSpec(memory_space=pl.ANY)

    message = (5, 2, 128)
    dealt = pl.pallas_call(
        deal_kernel,
        out_shape=jax.ShapeDtypeStruct((4, 4, NU) + message, jnp.bfloat16),
        in_specs=[anywhere, anywhere],
        out_specs=anywhere,
        scratch_shapes=[
            smem(structure.shape, jnp.int32),
            vmem(sigma.shape, jnp.bfloat16),
            vmem((NU,) + message, jnp.bfloat16),
            pltpu.SemaphoreType.DMA((2,)),
            pltpu.SemaphoreType.DMA((4, 4)),
        ],
        name="deal",
    )(structure, sigma)
    own = lax.all_to_all(dealt.reshape((NB * NB,) + message), CHIPS, 0, 0, tiled=True)
    flip = [(d, d ^ 1) for d in range(2 * NB * NB)]
    other = lax.ppermute(own, AXES, flip)
    names = own[:, 4, 0, : 2 * S].astype(jnp.int32).reshape(NB * NB * 2 * S)
    chosen, far = pl.pallas_call(
        pick_kernel,
        out_shape=(
            jax.ShapeDtypeStruct((NU, 16 * len(ORDER), 128), jnp.bfloat16),
            jax.ShapeDtypeStruct((8, 128), jnp.float32),
        ),
        in_specs=[scalars, whole, whole],
        out_specs=(whole, whole),
        compiler_params=pltpu.CompilerParams(vmem_limit_bytes=6 << 20),
        name="pick",
    )(names, own, other)
    picked = lax.all_to_all(chosen, NEAR, 0, 0, tiled=True)

    off, variance = pl.pallas_call(
        product_kernel,
        out_shape=(
            jax.ShapeDtypeStruct(factor.shape, jnp.bfloat16),
            jax.ShapeDtypeStruct(diag.shape, jnp.float32),
        ),
        in_specs=[scalars, whole, whole, whole, whole],
        out_specs=(anywhere, whole),
        scratch_shapes=[
            vmem((1024, 1024), jnp.bfloat16),
            vmem((S, 256, 1024), jnp.bfloat16),
            pltpu.SemaphoreType.DMA((S,)),
        ],
        compiler_params=pltpu.CompilerParams(vmem_limit_bytes=24 << 20),
        name="product",
    )(structure, picked, far, factor, diag)
    return off, variance


def solution(mesh):
    fine = Mesh(mesh.devices.reshape(tuple(SIZES.values())), AXES)
    return jax.shard_map(
        body,
        mesh=fine,
        in_specs=(
            P(AXES[:3], AXES[3:]),
            P(AXES, None),
            P(AXES, None, None),
            P(AXES, None),
        ),
        out_specs=(P(AXES, None, None), P(AXES, None)),
        check_vma=False,
    )
```

```python
import jax
import jax.numpy as jnp
from jax import lax
from jax.experimental import pallas as pl
from jax.experimental.pallas import tpu as pltpu
from jax.sharding import Mesh, PartitionSpec as P

SIZES = dict(yh=4, yl=2, xh=2, zh=4, zl=2, xl=2, c=2)
AXES = tuple(SIZES)
NEAR = ("yl", "zl", "xh", "xl")
CHIPS = ("yh", "zh") + NEAR
NB = 16
NU = 16
S = 4
PAIRS = [(k, l) for k in range(S) for l in range(k + 1, S)]
ORDER = [q for k, l in PAIRS for q in ((k, l), (l, k))] + [(k, k) for k in range(S)]


def iota(shape, dim):
    return lax.broadcasted_iota(jnp.int32, shape, dim)


def apart(shape):
    return (iota(shape, len(shape) - 1) - iota(shape, len(shape) - 2)) & 127


def kept(distance, low):
    return ((distance - low) & 127) < 64


def place():
    yh, yl, xh, zh, zl, xl, core = (lax.axis_index(a) for a in AXES)
    near = 8 * yl + 4 * zl + 2 * xh + xl
    return 4 * yh + 2 * yl + xh, 4 * zh + 2 * zl + xl, core, 4 * yh + zh, near


def shares(n):
    high, middle, low = n >> 2, (n >> 1) & 1, n & 1
    return 64 * high + 8 * middle + 2 * low, 16 * high + 4 * middle + low


def deal_kernel(structure_hbm, sigma_hbm, dealt, structure, sigma, out, sems, out_sems):
    copies = [
        pltpu.make_async_copy(structure_hbm, structure, sems.at[0]),
        pltpu.make_async_copy(sigma_hbm, sigma, sems.at[1]),
    ]
    for copy in copies:
        copy.start()
    for copy in copies:
        copy.wait()
    r, b, core, _, _ = place()
    lane, row = iota((8, 128), 1), iota((8, 128), 0)
    extra = jnp.zeros((8, 128), jnp.float32)
    for k in range(S):
        for h, share in enumerate(shares(structure[0, k])):
            extra = jnp.where(lane == S * h + k, share.astype(jnp.float32), extra)
    start = pl.multiple_of(128 * core, 128)
    square = -sigma[pl.ds(start, 128), :].astype(jnp.float32)
    far = jnp.where(apart((128, 128)) == 64, square, 0.0)
    extra = jnp.where(row == 1, jnp.sum(far, axis=0, keepdims=True), extra)
    extra = extra[:2].astype(jnp.bfloat16)
    first = (lane < 64) == (core == 0)
    for u in range(NU):
        low = jnp.where(r == b, (u // 8 > core).astype(jnp.int32), (r > b).astype(jnp.int32))
        tiles = []
        for v in (2 * u, 2 * u + 1):
            tile = -sigma[pl.ds(8 * v, 8), :].astype(jnp.float32)
            keep = kept(lane - row - 8 * v, low)
            tiles.append(jnp.where(keep, tile, pltpu.roll(tile, 64, 1)))
        tile = jnp.where(first, *tiles)
        for j in range(4):
            out[u, j] = tile[2 * j : 2 * j + 2].astype(jnp.bfloat16)
        out[u, 4] = extra
    spread = [
        pltpu.make_async_copy(out, dealt.at[yh, zh], out_sems.at[yh, zh])
        for yh in range(4)
        for zh in range(4)
    ]
    for copy in spread:
        copy.start()
    for copy in spread:
        copy.wait()


def pick_kernel(names, own, other, out, far):
    _, _, core, box, near = place()
    west = iota((8, 128), 1) < 64

    def run(left, right):
        mine = (box * NU + near) * 2 * S
        for k in range(S):
            at = names[mine + k] + names[mine + S + k]
            for g, half in enumerate((left, right)):
                far[4 * g + k : 4 * g + k + 1, :] = half[at, 4].astype(jnp.float32)[1:2]

        def step(i, carry):
            for t in range(4):
                t = 4 * i + t
                first = (box * NU + t) * 2 * S
                name = [names[first + k] for k in range(2 * S)]
                for q, (k, l) in enumerate(ORDER):
                    at = (name[k] + name[S + l], pl.ds(0, 4))
                    one = left[at].astype(jnp.float32).reshape(8, 128)
                    two = right[at].astype(jnp.float32).reshape(8, 128)
                    both = [jnp.where(west, one, two), jnp.where(west, two, one)]
                    rows = pl.ds(16 * q, 16)
                    out[t, rows, :] = jnp.concatenate(both, axis=0).astype(jnp.bfloat16)
            return carry

        lax.fori_loop(0, NU // 4, step, 0)

    @pl.when(core == 0)
    def _():
        run(own, other)

    @pl.when(core != 0)
    def _():
        run(other, own)


def unfold(picked, q):
    half = picked[:, pl.ds(16 * q, 16), :].reshape(256, 128)
    swapped = pltpu.roll(half.astype(jnp.float32), 64, 1).astype(jnp.bfloat16)
    first = (iota((256, 128), 1) < 64) == (iota((256, 128), 0) % 16 < 8)
    return jnp.where(first, half, swapped), jnp.where(first, swapped, half)


def quarter(half, g, h):
    return half[h][128 * g : 128 * g + 128]


def product_kernel(
    structure, picked, far, factor, diag, off, variance, gram, staged, sems
):
    total = diag[...]
    copies = []
    gap = apart((128, 128))
    for k in range(S):
        rows = pl.ds(256 * k, 256)
        for l in range(k, S):
            if l == k:
                one = two = unfold(picked, ORDER.index((k, k)))
            else:
                one = unfold(picked, ORDER.index((k, l)))
                two = unfold(picked, ORDER.index((l, k)))
                low = (structure[0, k] > structure[0, l]).astype(jnp.int32)
            for g in range(2):
                for h in range(2):
                    keep = kept(gap, int(g > h) if l == k else low)
                    value = jnp.where(keep, quarter(one, g, h), quarter(two, h, g).T)
                    if l == k and g == h:
                        spare = jnp.broadcast_to(far[pl.ds(4 * g + k, 1), :], value.shape)
                        value = jnp.where(gap == 64, spare.astype(jnp.bfloat16), value)
                    down, across = pl.ds(256 * k + 128 * g, 128), pl.ds(256 * l + 128 * h, 128)
                    gram[down, across] = value
                    if l > k:
                        gram[across, down] = value.T
        if k % 2 == 0:
            continue
        half, rows = k // 2, pl.ds(512 * (k // 2), 512)
        product = jnp.dot(gram[rows, :], factor[0], preferred_element_type=jnp.float32)
        staged[half] = product.astype(jnp.bfloat16)
        copies.append(
            pltpu.make_async_copy(staged.at[half], off.at[0, rows], sems.at[half])
        )
        copies[half].start()
        total -= jnp.sum(
            factor[0, rows, :].astype(jnp.float32) * product, axis=0, keepdims=True
        )
    variance[...] = total
    for copy in copies:
        copy.wait()


def body(sigma, structure, factor, diag):
    vmem, smem = pltpu.VMEM, pltpu.SMEM
    whole = pl.BlockSpec(memory_space=vmem)
    scalars = pl.BlockSpec(memory_space=smem)
    anywhere = pl.BlockSpec(memory_space=pl.ANY)

    message = (5, 2, 128)
    dealt = pl.pallas_call(
        deal_kernel,
        out_shape=jax.ShapeDtypeStruct((4, 4, NU) + message, jnp.bfloat16),
        in_specs=[anywhere, anywhere],
        out_specs=anywhere,
        scratch_shapes=[
            smem(structure.shape, jnp.int32),
            vmem(sigma.shape, jnp.bfloat16),
            vmem((NU,) + message, jnp.bfloat16),
            pltpu.SemaphoreType.DMA((2,)),
            pltpu.SemaphoreType.DMA((4, 4)),
        ],
        name="deal",
    )(structure, sigma)
    own = lax.all_to_all(dealt.reshape((NB * NB,) + message), CHIPS, 0, 0, tiled=True)
    flip = [(d, d ^ 1) for d in range(2 * NB * NB)]
    other = lax.ppermute(own, AXES, flip)
    names = own[:, 4, 0, : 2 * S].astype(jnp.int32).reshape(NB * NB * 2 * S)
    chosen, far = pl.pallas_call(
        pick_kernel,
        out_shape=(
            jax.ShapeDtypeStruct((NU, 16 * len(ORDER), 128), jnp.bfloat16),
            jax.ShapeDtypeStruct((8, 128), jnp.float32),
        ),
        in_specs=[scalars, whole, whole],
        out_specs=(whole, whole),
        compiler_params=pltpu.CompilerParams(vmem_limit_bytes=6 << 20),
        name="pick",
    )(names, own, other)
    picked = lax.all_to_all(chosen, NEAR, 0, 0, tiled=True)

    off, variance = pl.pallas_call(
        product_kernel,
        out_shape=(
            jax.ShapeDtypeStruct(factor.shape, jnp.bfloat16),
            jax.ShapeDtypeStruct(diag.shape, jnp.float32),
        ),
        in_specs=[scalars, whole, whole, whole, whole],
        out_specs=(anywhere, whole),
        scratch_shapes=[
            vmem((1024, 1024), jnp.bfloat16),
            vmem((2, 512, 1024), jnp.bfloat16),
            pltpu.SemaphoreType.DMA((2,)),
        ],
        compiler_params=pltpu.CompilerParams(vmem_limit_bytes=24 << 20),
        name="product",
    )(structure, picked, far, factor, diag)
    return off, variance


def solution(mesh):
    fine = Mesh(mesh.devices.reshape(tuple(SIZES.values())), AXES)
    return jax.shard_map(
        body,
        mesh=fine,
        in_specs=(
            P(AXES[:3], AXES[3:]),
            P(AXES, None),
            P(AXES, None, None),
            P(AXES, None),
        ),
        out_specs=(P(AXES, None, None), P(AXES, None)),
        check_vma=False,
    )
```
